32 devices in a mesh: aux: 4 (over y, x), blk: 8 (over z, core).
Axes of the slice: x: 2, y: 2, z: 4, core: 2. Of those that a mesh axis runs over, the one named last changes fastest.
Arguments:
- integrals: bfloat16 [2048, 64, 1024], P(('aux', 'blk')), may hold values from -0.5 to 0.5
- metric: bfloat16 [2048, 512], P('aux'), may hold values from -1 to 2
- pair_list: int32 [15, 2], replicated, may hold values from 0 to 7, as said below
- aux_mask: int32 [16, 8], P('aux'), may hold values 0 or 1
Outputs:
- band_rows: float32 [8, 128, 640], P('blk', 'aux')
The draws below stay inside these ranges and needn't reach their ends.
Inputs may be any that keep to these rules, and one draw needn't show every extreme that they name: `pair_list`: every pair (r, r) appears once; the other rows are distinct pairs (r, r + 1) or (r, r + 2) with both blocks below 8; 7 such rows.
All inputs are finite; a program needn't handle non-finite values. No bound on the sum of `aux_mask` on one device may be relied on, other than what follows from the above.
Results may differ from the reference program's by a relative error of at most 0.0015.
Values may be sent and summed in bfloat16 or wider, within the bound.
A program may use at most 128 MiB of HBM per device.

```python
import math
import jax
import jax.numpy as jnp
from jax import lax

NOCC = 64
QSH = 512
BS = 128
QB = 128
SPAN = 3
NAUX = 2048
NBLK = 8
NQB = 16
N_AUX = 4


def draw_metric(key, part):
    noise_part = jax.random.normal(key, (NAUX, QSH), jnp.float32)
    noise_part = jnp.clip(noise_part, -4.0, 4.0) * (0.5 / math.sqrt(QSH))
    identity = jnp.tile(jnp.eye(QSH, dtype=jnp.float32), (NAUX // QSH, 1))
    return (identity + noise_part).astype(jnp.bfloat16)


def draw_pair_list(key, part):
    first_ids = jnp.arange(NBLK - 1, dtype=jnp.int32)
    second_ids = jnp.arange(NBLK - 2, dtype=jnp.int32)
    rows_off = jnp.concatenate([first_ids, second_ids])
    cols_off = jnp.concatenate([first_ids + 1, second_ids + 2])
    chosen = jax.random.permutation(jax.random.fold_in(key, 11), 2 * NBLK - 3)[:NBLK - 1]
    diagonal = jnp.arange(NBLK, dtype=jnp.int32)
    row_ids = jnp.concatenate([diagonal, rows_off[chosen]])
    col_ids = jnp.concatenate([diagonal, cols_off[chosen]])
    return jnp.stack([row_ids, col_ids], axis=1).astype(jnp.int32)


def plant(drawn, key, low, high):
    longest = drawn.shape.index(max(drawn.shape))
    spots = []
    for shift in (0, 1):
        where = [jax.random.randint(jax.random.fold_in(key, axis), (), 0, length) for axis, length in enumerate(drawn.shape)]
        where[longest] = (where[longest] + shift) % drawn.shape[longest]
        spots.append(tuple(where))
    return drawn.at[spots[0]].set(low).at[spots[1]].set(high)


def steps_of(rng, extent, cuts, low, top_value):
    def one(dim, blocks):
        steps = jax.random.uniform(jax.random.fold_in(jax.random.fold_in(rng, 6), dim), (blocks,), jnp.float32, low / len(cuts), top_value / len(cuts))
        return jnp.repeat(jnp.exp(steps), extent[dim] // blocks).reshape((-1,) + (1,) * (len(extent) - dim - 1))

    loudness = one(*cuts[0])
    for cut in cuts[1:]:
        loudness = loudness * one(*cut)
    return loudness


def normal_values(own_key, extent, spread, bound, cuts=(), kind=jnp.bfloat16):
    array = jax.random.normal(own_key, extent, jnp.float32) * spread
    if len(cuts) > 0:
        array = steps_of(own_key, extent, cuts, -0.22, 0.18) * array
    return jnp.clip(array, min=-bound, max=bound).astype(kind)


def setup_inputs(seed: int = 0) -> dict:
    keys = jax.random.split(jax.random.key(seed), 5)
    integrals = normal_values(keys[0], (NAUX, NOCC, NBLK * BS), 0.07, 0.5, ((0, 32),))
    metric = draw_metric(jax.random.fold_in(keys[4], 71), 0)
    pair_list = draw_pair_list(jax.random.fold_in(keys[4], 71), 0)
    aux_mask = plant((jax.random.randint(keys[3], (NQB, NBLK), 0, 4) < 3).astype(jnp.int32), jax.random.fold_in(keys[3], 1), 0, 1)
    return {"integrals": integrals, "metric": metric, "pair_list": pair_list, "aux_mask": aux_mask}


def fit_all(integrals, metric, aux_mask):
    domains = metric.reshape(N_AUX, QSH, QSH).astype(jnp.float32)
    row_masks = jnp.repeat(aux_mask, QB, axis=0).astype(jnp.float32)

    def fit_one(block_id):
        columns = lax.dynamic_slice_in_dim(integrals, block_id * BS, BS, 2).astype(jnp.float32)
        columns = columns.reshape(N_AUX, QSH, NOCC, BS)
        fitted = jnp.einsum("apq,aqin->apin", domains, columns).reshape(NAUX, NOCC, BS)
        keep_rows = lax.dynamic_slice_in_dim(row_masks, block_id, 1, 1)
        return (fitted * keep_rows[:, :, None]).astype(jnp.bfloat16)

    return lax.map(fit_one, jnp.arange(NBLK, dtype=jnp.int32))


def reference(integrals, metric, pair_list, aux_mask):
    fitted = fit_all(integrals, metric, aux_mask)
    block_ids = jnp.arange(NBLK, dtype=jnp.int32)
    offsets = jnp.arange(SPAN, dtype=jnp.int32)
    col_gap = pair_list[:, 1] - pair_list[:, 0]
    hits = (pair_list[:, 0][:, None, None] == block_ids[None, :, None]) & (col_gap[:, None, None] == offsets[None, None, :])
    listed = jnp.sum(hits.astype(jnp.int32), axis=0).astype(jnp.float32)

    def row_tiles(block_id):
        own_block = fitted[block_id].reshape(-1, BS).astype(jnp.float32)
        tile_list = []
        for distance in range(SPAN):
            partner_id = jnp.minimum(block_id + distance, NBLK - 1)
            partner = fitted[partner_id].reshape(-1, BS).astype(jnp.float32)
            tile_list.append(lax.dot_general(own_block, partner, (((0,), (0,)), ((), ())), preferred_element_type=jnp.float32))
        return jnp.stack(tile_list)

    upper_tiles = lax.map(row_tiles, block_ids) * listed[:, :, None, None]
    pieces = []
    for column_slot in range(2 * SPAN - 1):
        offset = column_slot - (SPAN - 1)
        if offset >= 0:
            pieces.append(upper_tiles[:, offset])
        else:
            distance = -offset
            shifted = jnp.concatenate([jnp.zeros((distance, BS, BS), jnp.float32), upper_tiles[: NBLK - distance, distance]], axis=0)
            pieces.append(jnp.swapaxes(shifted, 1, 2))
    return jnp.concatenate(pieces, axis=2)
```

```python
import functools

import jax
import jax.numpy as jnp
from jax import lax
from jax.experimental import pallas as pl
from jax.experimental.pallas import tpu as pltpu
from jax.sharding import PartitionSpec as P

BS = 128
QB = 128
SPAN = 3
SUB = 8
MESH = pl.DeviceIdType.MESH


def listed_of(pair_list, block_count):
    block_ids = jnp.arange(block_count, dtype=jnp.int32)
    offsets = jnp.arange(SPAN, dtype=jnp.int32)
    col_gap = pair_list[:, 1] - pair_list[:, 0]
    hits = (pair_list[:, 0][:, None, None] == block_ids[None, :, None]) & (
        col_gap[:, None, None] == offsets[None, None, :]
    )
    return jnp.sum(hits.astype(jnp.int32), axis=0)


def tile_kernel(
    peers, blocks, depth, mask_ref, metric_ref, x_ref, out_ref,
    slab, wide, ordered, fit_rows, fit_cols, send_sem, recv_sem, own_sem,
):
    me = lax.axis_index("blk")
    rows = depth // peers

    barrier = pltpu.get_barrier_semaphore()

    def greet(off, carry):
        pl.semaphore_signal(
            barrier, inc=1, device_id={"blk": lax.rem(me + off, peers)}, device_id_type=MESH
        )
        return carry

    lax.fori_loop(1, peers, greet, 0)
    pl.semaphore_wait(barrier, peers - 1)

    def source(block, target):
        return x_ref.at[
            :,
            pl.ds(pl.multiple_of(target * SUB, SUB), SUB),
            pl.ds(pl.multiple_of(block * BS, BS), BS),
        ]

    def landing(block, sender):
        return slab.at[block, pl.ds(pl.multiple_of(sender * rows, rows), rows)]

    def outgoing(block, off):
        target = lax.rem(me + off, peers)
        return pltpu.make_async_remote_copy(
            src_ref=source(block, target),
            dst_ref=landing(block, me),
            send_sem=send_sem.at[block, off],
            recv_sem=recv_sem.at[block, off],
            device_id={"blk": target},
            device_id_type=MESH,
        )

    def incoming(block, off):
        sender = lax.rem(me - off + peers, peers)
        return pltpu.make_async_remote_copy(
            src_ref=source(block, me),
            dst_ref=landing(block, sender),
            send_sem=send_sem.at[block, off],
            recv_sem=recv_sem.at[block, off],
            device_id={"blk": sender},
            device_id_type=MESH,
        )

    def own(block):
        return pltpu.make_async_copy(source(block, me), landing(block, me), own_sem.at[block])

    def launch(block, carry):
        def one(off, inner):
            outgoing(block, off).start()
            return inner

        lax.fori_loop(1, peers, one, 0)
        own(block).start()
        return carry

    lax.fori_loop(0, blocks, launch, 0)

    fit_cols[: (SPAN - 1) * BS, :] = jnp.zeros(((SPAN - 1) * BS, SUB * depth), jnp.bfloat16)

    def step(block, carry):
        def arrive(off, inner):
            incoming(block, off).wait_recv()
            return inner

        lax.fori_loop(1, peers, arrive, 0)
        own(block).wait()
        wide[...] = slab[block].reshape(depth * SUB, BS).astype(jnp.float32)
        for i in range(SUB):
            ordered[:, i * BS : (i + 1) * BS] = wide[pl.ds(i, depth, stride=SUB), :].astype(
                jnp.bfloat16
            )
        for qb in range(depth // QB):
            keep = mask_ref[qb, block].astype(jnp.float32)
            fitted = jnp.dot(
                metric_ref[qb * QB : (qb + 1) * QB, :],
                ordered[...],
                preferred_element_type=jnp.float32,
            )
            fitted = fitted * keep
            for i in range(SUB):
                piece = fitted[:, i * BS : (i + 1) * BS]
                at = i * depth + qb * QB
                fit_rows[at : at + QB, :] = piece.astype(jnp.bfloat16)
                fit_cols[
                    pl.ds(pl.multiple_of((block + SPAN - 1) * BS, BS), BS), at : at + QB
                ] = piece.T.astype(jnp.bfloat16)
        out_ref[block] = jnp.dot(
            fit_cols[pl.ds(pl.multiple_of(block * BS, BS), SPAN * BS), :],
            fit_rows[...],
            preferred_element_type=jnp.float32,
        )
        return carry

    lax.fori_loop(0, blocks, step, 0)

    def settle(block, carry):
        def one(off, inner):
            outgoing(block, off).wait_send()
            return inner

        lax.fori_loop(1, peers, one, 0)
        return carry

    lax.fori_loop(0, blocks, settle, 0)


def partial_tiles(integrals, metric, aux_mask, peers):
    depth = metric.shape[1]
    blocks = aux_mask.shape[1]
    return pl.pallas_call(
        functools.partial(tile_kernel, peers, blocks, depth),
        out_shape=jax.ShapeDtypeStruct((blocks, SPAN * BS, BS), jnp.float32),
        in_specs=[
            pl.BlockSpec(memory_space=pltpu.SMEM),
            pl.BlockSpec(memory_space=pltpu.VMEM),
            pl.BlockSpec(memory_space=pl.ANY),
        ],
        out_specs=pl.BlockSpec(memory_space=pltpu.VMEM),
        scratch_shapes=[
            pltpu.VMEM((blocks, depth, SUB, BS), jnp.bfloat16),
            pltpu.VMEM((depth * SUB, BS), jnp.float32),
            pltpu.VMEM((depth, SUB * BS), jnp.bfloat16),
            pltpu.VMEM((SUB * depth, BS), jnp.bfloat16),
            pltpu.VMEM(((blocks + SPAN - 1) * BS, SUB * depth), jnp.bfloat16),
            pltpu.SemaphoreType.DMA((blocks, peers)),
            pltpu.SemaphoreType.DMA((blocks, peers)),
            pltpu.SemaphoreType.DMA((blocks,)),
        ],
        compiler_params=pltpu.CompilerParams(
            collective_id=0, has_side_effects=True, vmem_limit_bytes=60 * 1024 * 1024
        ),
    )(aux_mask, metric, integrals)


def by_orbital(integrals, metric, pair_list, aux_mask):
    peers = lax.axis_size("blk")
    blocks = aux_mask.shape[1]
    listed = listed_of(pair_list, blocks).astype(jnp.float32)
    parts = partial_tiles(integrals, metric, aux_mask, peers)
    parts = parts.reshape(blocks, SPAN, BS, BS)
    pieces = []
    for slot in range(2 * SPAN - 1):
        offset = slot - (SPAN - 1)
        if offset < 0:
            weight = jnp.pad(listed[: blocks + offset, -offset], (-offset, 0))
            tile = jnp.swapaxes(parts[:, SPAN - 1 + offset], 1, 2)
        else:
            weight = listed[:, offset]
            tile = jnp.pad(parts[offset:, SPAN - 1 - offset], ((0, offset), (0, 0), (0, 0)))
        pieces.append(tile * weight[:, None, None])
    band = jnp.concatenate(pieces, axis=2)
    band = lax.psum_scatter(band, "aux", scatter_dimension=1, tiled=True)
    return lax.psum_scatter(band, "blk", scatter_dimension=0, tiled=True)


def from_behind(array, axis, by):
    peers = lax.axis_size(axis)
    pairs = [(i, i + by) for i in range(peers) if 0 <= i + by < peers]
    return lax.ppermute(array, axis, pairs)


def fit_block(metric, slab_piece, mask_rows):
    fitted = jnp.einsum("pq,qjn->pjn", metric, slab_piece, preferred_element_type=jnp.float32)
    return (fitted * mask_rows[:, None, None]).astype(jnp.bfloat16)


def by_block(integrals, metric, pair_list, aux_mask):
    block_count = aux_mask.shape[1]
    position = lax.axis_index("blk")
    block_ids = jnp.arange(block_count, dtype=jnp.int32)
    offsets = jnp.arange(SPAN, dtype=jnp.int32)
    col_gap = pair_list[:, 1] - pair_list[:, 0]
    hits = (pair_list[:, 0][:, None] == position) & (col_gap[:, None] == offsets[None, :])
    listed = jnp.sum(hits.astype(jnp.int32), axis=0)
    one_hot = (block_ids == position).astype(jnp.int32)
    column = jnp.sum(aux_mask * one_hot[None, :], axis=1)
    own_mask = jnp.repeat(column, QB).astype(jnp.float32)
    own_block = fit_block(
        metric, lax.all_to_all(integrals, "blk", split_axis=2, concat_axis=0, tiled=True), own_mask
    )
    partners = [own_block]
    current = own_block
    for turn_index in range(SPAN - 1):
        current = from_behind(current, "blk", -1)
        partners.append(current)
    flat_own = partners[0].reshape(-1, BS)

    def make_tile(partner):
        return lax.dot_general(
            flat_own,
            partner.reshape(-1, BS),
            (((0,), (0,)), ((), ())),
            preferred_element_type=jnp.float32,
        )

    tile_list = [
        make_tile(partners[offset]) * listed[offset].astype(jnp.float32) for offset in range(SPAN)
    ]
    upper_tiles = jnp.stack(tile_list)
    mirror_tiles = jnp.stack([jnp.transpose(tile_list[offset]) for offset in range(1, SPAN)])
    lower_tiles = []
    moving = mirror_tiles
    for turn_index in range(SPAN - 1):
        moving = from_behind(moving.astype(jnp.bfloat16), "blk", 1).astype(moving.dtype)
        lower_tiles.append(moving[0])
        moving = moving[1:]
    whole_band = jnp.concatenate(
        [jnp.stack([lower_tiles[SPAN - 2 - slot] for slot in range(SPAN - 1)]), upper_tiles], axis=0
    )
    band_parts = lax.psum_scatter(whole_band, "aux", scatter_dimension=1, tiled=True)
    pieces = [band_parts[slot] for slot in range(2 * SPAN - 1)]
    band_rows = jnp.concatenate(pieces, axis=1)
    return band_rows[None]


def local(integrals, metric, pair_list, aux_mask):
    peers = lax.axis_size("blk")
    blocks = aux_mask.shape[1]
    whole_tiles = integrals.shape[1] == SUB * peers and blocks == peers
    if whole_tiles:
        return by_orbital(integrals, metric, pair_list, aux_mask)
    return by_block(integrals, metric, pair_list, aux_mask)


def solution(mesh):
    return jax.shard_map(
        local,
        mesh=mesh,
        in_specs=(P(("aux", "blk"), None, None), P("aux", None), P(), P("aux", None)),
        out_specs=P("blk", "aux", None),
        check_vma=False,
    )
```

```python
import functools

import jax
import jax.numpy as jnp
from jax import lax
from jax.experimental import pallas as pl
from jax.experimental.pallas import tpu as pltpu
from jax.sharding import PartitionSpec as P

BS = 128
QB = 128
SPAN = 3
SUB = 8
PAIR = 2
MESH = pl.DeviceIdType.MESH


def tile_kernel(
    peers, domains, blocks, depth, mask_ref, pairs_ref, metric_ref, x_ref, out_ref,
    slab, wide, ordered, fit_rows, fit_cols, piece_out, piece_in, sum_out, sum_in, weights,
    send_sem, recv_sem, own_sem, piece_send, piece_recv, sum_send, sum_recv,
):
    me = lax.axis_index("blk")
    domain = lax.axis_index("aux")
    rows = depth // peers
    group = domains * PAIR
    strip = BS // group
    pair_base = (me // PAIR) * PAIR
    place = domain * PAIR + lax.rem(me, PAIR)
    slots = 2 * SPAN - 1

    barrier = pltpu.get_barrier_semaphore()

    def member(off):
        other = lax.rem(place + off, group)
        return {"aux": other // PAIR, "blk": pair_base + lax.rem(other, PAIR)}

    def greet(off, carry):
        pl.semaphore_signal(
            barrier, inc=1, device_id={"blk": lax.rem(me + off, peers)}, device_id_type=MESH
        )
        return carry

    lax.fori_loop(1, peers, greet, 0)
    for turn in range(1, domains):
        for core in range(PAIR):
            pl.semaphore_signal(
                barrier,
                inc=1,
                device_id={"aux": lax.rem(domain + turn, domains), "blk": pair_base + core},
                device_id_type=MESH,
            )
    pl.semaphore_wait(barrier, peers - 1 + (domains - 1) * PAIR)

    def source(block, target):
        return x_ref.at[
            :,
            pl.ds(pl.multiple_of(target * SUB, SUB), SUB),
            pl.ds(pl.multiple_of(block * BS, BS), BS),
        ]

    def landing(block, sender):
        return slab.at[block, pl.ds(pl.multiple_of(sender * rows, rows), rows)]

    def outgoing(block, off):
        target = lax.rem(me + off, peers)
        return pltpu.make_async_remote_copy(
            src_ref=source(block, target),
            dst_ref=landing(block, me),
            send_sem=send_sem.at[block, off],
            recv_sem=recv_sem.at[block, off],
            device_id={"blk": target},
            device_id_type=MESH,
        )

    def incoming(block, off):
        sender = lax.rem(me - off + peers, peers)
        return pltpu.make_async_remote_copy(
            src_ref=source(block, me),
            dst_ref=landing(block, sender),
            send_sem=send_sem.at[block, off],
            recv_sem=recv_sem.at[block, off],
            device_id={"blk": sender},
            device_id_type=MESH,
        )

    def own(block):
        return pltpu.make_async_copy(source(block, me), landing(block, me), own_sem.at[block])

    def launch(block, carry):
        def one(off, inner):
            outgoing(block, off).start()
            return inner

        lax.fori_loop(1, peers, one, 0)
        own(block).start()
        return carry

    lax.fori_loop(0, blocks, launch, 0)

    for slot in range(slots):
        gap = abs(slot - (SPAN - 1))
        row = me if slot >= SPAN - 1 else me - gap
        count = jnp.int32(0)
        for index in range(pairs_ref.shape[0]):
            first = pairs_ref[index, 0]
            hit = (first == row) & (pairs_ref[index, 1] - first == gap)
            count = count + hit.astype(jnp.int32)
        weights[slot] = count.astype(jnp.float32)

    fit_cols[: (SPAN - 1) * BS, :] = jnp.zeros(((SPAN - 1) * BS, SUB * depth), jnp.bfloat16)
    for gap in range(1, SPAN):

        @pl.when(me + gap >= blocks)
        def _():
            sum_in[:, SPAN - 1 + gap] = jnp.zeros((peers, strip, BS), jnp.float32)

    def piece_to(block, off):
        return pltpu.make_async_remote_copy(
            src_ref=piece_out.at[block, lax.rem(place + off, group)],
            dst_ref=piece_in.at[block, place],
            send_sem=piece_send.at[block, off],
            recv_sem=piece_recv.at[block, off],
            device_id=member(off),
            device_id_type=MESH,
        )

    def piece_from(block, off):
        sender = lax.rem(place - off + group, group)
        return pltpu.make_async_remote_copy(
            src_ref=piece_out.at[block, sender],
            dst_ref=piece_in.at[block, sender],
            send_sem=piece_send.at[block, off],
            recv_sem=piece_recv.at[block, off],
            device_id=member(group - off),
            device_id_type=MESH,
        )

    def span_of(gap):
        return pl.ds(0, SPAN) if gap == 0 else pl.ds(SPAN - 1 + gap, 1)

    def sum_to(block, gap):
        return pltpu.make_async_remote_copy(
            src_ref=sum_out.at[block, span_of(gap)],
            dst_ref=sum_in.at[me, span_of(gap)],
            send_sem=sum_send.at[block, gap],
            recv_sem=sum_recv.at[me, gap],
            device_id={"blk": block - gap},
            device_id_type=MESH,
        )

    def sum_from(sender, gap):
        return pltpu.make_async_remote_copy(
            src_ref=sum_out.at[0, span_of(gap)],
            dst_ref=sum_in.at[sender, span_of(gap)],
            send_sem=sum_send.at[0, gap],
            recv_sem=sum_recv.at[sender, gap],
            device_id={"blk": sender},
            device_id_type=MESH,
        )

    def pass_on(block):
        def arrive(off, inner):
            piece_from(block, off).wait_recv()
            return inner

        lax.fori_loop(1, group, arrive, 0)
        total = piece_out[block, place]
        for off in range(1, group):
            total = total + piece_in[block, lax.rem(place + off, group)]
        sum_out[block] = total
        for gap in range(SPAN):
            owner = block - gap

            @pl.when((owner >= 0) & (owner != me))
            def _():
                sum_to(block, gap).start()

            @pl.when(owner == me)
            def _():
                if gap == 0:
                    sum_in[me, :SPAN] = total[:SPAN]
                else:
                    sum_in[me, SPAN - 1 + gap] = total[SPAN - 1 + gap]

    def step(block, carry):
        @pl.when(block > 0)
        def _():
            pass_on(block - 1)

        def arrive(off, inner):
            incoming(block, off).wait_recv()
            return inner

        lax.fori_loop(1, peers, arrive, 0)
        own(block).wait()
        wide[...] = slab[block].reshape(depth * SUB, BS).astype(jnp.float32)
        for i in range(SUB):
            ordered[:, i * BS : (i + 1) * BS] = wide[pl.ds(i, depth, stride=SUB), :].astype(
                jnp.bfloat16
            )
        for qb in range(depth // QB):
            keep = mask_ref[qb, block].astype(jnp.float32)
            fitted = jnp.dot(
                metric_ref[qb * QB : (qb + 1) * QB, :],
                ordered[...],
                preferred_element_type=jnp.float32,
            )
            fitted = fitted * keep
            for i in range(SUB):
                piece = fitted[:, i * BS : (i + 1) * BS]
                at = i * depth + qb * QB
                fit_rows[at : at + QB, :] = piece.astype(jnp.bfloat16)
                fit_cols[
                    pl.ds(pl.multiple_of((block + SPAN - 1) * BS, BS), BS), at : at + QB
                ] = piece.T.astype(jnp.bfloat16)
        tiles = jnp.dot(
            fit_cols[pl.ds(pl.multiple_of(block * BS, BS), SPAN * BS), :],
            fit_rows[...],
            preferred_element_type=jnp.float32,
        )
        for gap in range(SPAN):
            at = (SPAN - 1 - gap) * BS
            tile = tiles[at : at + BS, :]
            piece_out[block, :, SPAN - 1 + gap] = tile.reshape(group, strip, BS)
            if gap > 0:
                piece_out[block, :, SPAN - 1 - gap] = tile.T.reshape(group, strip, BS)

        def one(off, inner):
            piece_to(block, off).start()
            return inner

        lax.fori_loop(1, group, one, 0)
        return carry

    lax.fori_loop(0, blocks, step, 0)
    pass_on(blocks - 1)

    for gap in range(SPAN):

        @pl.when(me + gap < blocks)
        def _():
            def arrive(off, inner):
                sum_from(lax.rem(me + off, peers), gap).wait_recv()
                return inner

            lax.fori_loop(1, peers, arrive, 0)

    for core in range(PAIR):
        for slot in range(slots):
            total = sum_in[core, slot]
            for turn in range(1, peers // PAIR):
                total = total + sum_in[turn * PAIR + core, slot]
            out_ref[0, core * strip : (core + 1) * strip, slot * BS : (slot + 1) * BS] = (
                total * weights[slot]
            )

    def settle(block, carry):
        def one(off, inner):
            outgoing(block, off).wait_send()
            return inner

        def two(off, inner):
            piece_to(block, off).wait_send()
            return inner

        lax.fori_loop(1, peers, one, 0)
        lax.fori_loop(1, group, two, 0)
        for gap in range(SPAN):
            owner = block - gap

            @pl.when((owner >= 0) & (owner != me))
            def _():
                sum_to(block, gap).wait_send()

        return carry

    lax.fori_loop(0, blocks, settle, 0)


def by_orbital(integrals, metric, pair_list, aux_mask):
    peers = lax.axis_size("blk")
    domains = lax.axis_size("aux")
    depth = metric.shape[1]
    blocks = aux_mask.shape[1]
    group = domains * PAIR
    slots = 2 * SPAN - 1
    strip = BS // group
    return pl.pallas_call(
        functools.partial(tile_kernel, peers, domains, blocks, depth),
        out_shape=jax.ShapeDtypeStruct((1, BS // domains, slots * BS), jnp.float32),
        in_specs=[
            pl.BlockSpec(memory_space=pltpu.SMEM),
            pl.BlockSpec(memory_space=pltpu.SMEM),
            pl.BlockSpec(memory_space=pltpu.VMEM),
            pl.BlockSpec(memory_space=pl.ANY),
        ],
        out_specs=pl.BlockSpec(memory_space=pltpu.VMEM),
        scratch_shapes=[
            pltpu.VMEM((blocks, depth, SUB, BS), jnp.bfloat16),
            pltpu.VMEM((depth * SUB, BS), jnp.float32),
            pltpu.VMEM((depth, SUB * BS), jnp.bfloat16),
            pltpu.VMEM((SUB * depth, BS), jnp.bfloat16),
            pltpu.VMEM(((blocks + SPAN - 1) * BS, SUB * depth), jnp.bfloat16),
            pltpu.VMEM((blocks, group, slots, strip, BS), jnp.float32),
            pltpu.VMEM((blocks, group, slots, strip, BS), jnp.float32),
            pltpu.VMEM((blocks, slots, strip, BS), jnp.float32),
            pltpu.VMEM((peers, slots, strip, BS), jnp.float32),
            pltpu.SMEM((slots,), jnp.float32),
            pltpu.SemaphoreType.DMA((blocks, peers)),
            pltpu.SemaphoreType.DMA((blocks, peers)),
            pltpu.SemaphoreType.DMA((blocks,)),
            pltpu.SemaphoreType.DMA((blocks, group)),
            pltpu.SemaphoreType.DMA((blocks, group)),
            pltpu.SemaphoreType.DMA((blocks, SPAN)),
            pltpu.SemaphoreType.DMA((peers, SPAN)),
        ],
        compiler_params=pltpu.CompilerParams(
            collective_id=0, has_side_effects=True, vmem_limit_bytes=60 * 1024 * 1024
        ),
    )(aux_mask, pair_list, metric, integrals)


def from_behind(array, axis, by):
    peers = lax.axis_size(axis)
    pairs = [(i, i + by) for i in range(peers) if 0 <= i + by < peers]
    return lax.ppermute(array, axis, pairs)


def fit_block(metric, slab_piece, mask_rows):
    fitted = jnp.einsum("pq,qjn->pjn", metric, slab_piece, preferred_element_type=jnp.float32)
    return (fitted * mask_rows[:, None, None]).astype(jnp.bfloat16)


def by_block(integrals, metric, pair_list, aux_mask):
    block_count = aux_mask.shape[1]
    position = lax.axis_index("blk")
    block_ids = jnp.arange(block_count, dtype=jnp.int32)
    offsets = jnp.arange(SPAN, dtype=jnp.int32)
    col_gap = pair_list[:, 1] - pair_list[:, 0]
    hits = (pair_list[:, 0][:, None] == position) & (col_gap[:, None] == offsets[None, :])
    listed = jnp.sum(hits.astype(jnp.int32), axis=0)
    one_hot = (block_ids == position).astype(jnp.int32)
    column = jnp.sum(aux_mask * one_hot[None, :], axis=1)
    own_mask = jnp.repeat(column, QB).astype(jnp.float32)
    own_block = fit_block(
        metric, lax.all_to_all(integrals, "blk", split_axis=2, concat_axis=0, tiled=True), own_mask
    )
    partners = [own_block]
    current = own_block
    for turn_index in range(SPAN - 1):
        current = from_behind(current, "blk", -1)
        partners.append(current)
    flat_own = partners[0].reshape(-1, BS)

    def make_tile(partner):
        return lax.dot_general(
            flat_own,
            partner.reshape(-1, BS),
            (((0,), (0,)), ((), ())),
            preferred_element_type=jnp.float32,
        )

    tile_list = [
        make_tile(partners[offset]) * listed[offset].astype(jnp.float32) for offset in range(SPAN)
    ]
    upper_tiles = jnp.stack(tile_list)
    mirror_tiles = jnp.stack([jnp.transpose(tile_list[offset]) for offset in range(1, SPAN)])
    lower_tiles = []
    moving = mirror_tiles
    for turn_index in range(SPAN - 1):
        moving = from_behind(moving.astype(jnp.bfloat16), "blk", 1).astype(moving.dtype)
        lower_tiles.append(moving[0])
        moving = moving[1:]
    whole_band = jnp.concatenate(
        [jnp.stack([lower_tiles[SPAN - 2 - slot] for slot in range(SPAN - 1)]), upper_tiles], axis=0
    )
    band_parts = lax.psum_scatter(whole_band, "aux", scatter_dimension=1, tiled=True)
    pieces = [band_parts[slot] for slot in range(2 * SPAN - 1)]
    band_rows = jnp.concatenate(pieces, axis=1)
    return band_rows[None]


def local(integrals, metric, pair_list, aux_mask):
    peers = lax.axis_size("blk")
    blocks = aux_mask.shape[1]
    strips = BS % (8 * PAIR * lax.axis_size("aux")) == 0 and peers % PAIR == 0
    whole_tiles = integrals.shape[1] == SUB * peers and blocks == peers and strips
    if whole_tiles:
        return by_orbital(integrals, metric, pair_list, aux_mask)
    return by_block(integrals, metric, pair_list, aux_mask)


def solution(mesh):
    return jax.shard_map(
        local,
        mesh=mesh,
        in_specs=(P(("aux", "blk"), None, None), P("aux", None), P(), P("aux", None)),
        out_specs=P("blk", "aux", None),
        check_vma=False,
    )
```

```python
import functools

import jax
import jax.numpy as jnp
from jax import lax
from jax.experimental import pallas as pl
from jax.experimental.pallas import tpu as pltpu
from jax.sharding import PartitionSpec as P

BS = 128
QB = 128
SPAN = 3
SUB = 8
PAIR = 2
MESH = pl.DeviceIdType.MESH


def tile_kernel(
    peers, domains, blocks, depth, mask_hbm, pairs_hbm, metric_hbm, x_ref, out_ref,
    mask_ref, pairs_ref, metric_ref,
    slab, wide, ordered, fit_rows, fit_cols, piece_out, piece_in, sum_out, sum_in, weights,
    send_sem, recv_sem, own_sem, piece_send, piece_recv, sum_send, sum_recv, load_sem,
):
    me = lax.axis_index("blk")
    domain = lax.axis_index("aux")
    rows = depth // peers
    group = domains * PAIR
    strip = BS // group
    pair_base = (me // PAIR) * PAIR
    place = domain * PAIR + lax.rem(me, PAIR)
    slots = 2 * SPAN - 1

    loads = [
        pltpu.make_async_copy(mask_hbm, mask_ref, load_sem.at[0]),
        pltpu.make_async_copy(pairs_hbm, pairs_ref, load_sem.at[1]),
        pltpu.make_async_copy(metric_hbm, metric_ref, load_sem.at[2]),
    ]
    for load in loads:
        load.start()
    barrier = pltpu.get_barrier_semaphore()

    def member(off):
        other = lax.rem(place + off, group)
        return {"aux": other // PAIR, "blk": pair_base + lax.rem(other, PAIR)}

    def greet(off, carry):
        pl.semaphore_signal(
            barrier, inc=1, device_id={"blk": lax.rem(me + off, peers)}, device_id_type=MESH
        )
        return carry

    lax.fori_loop(1, peers, greet, 0)
    for turn in range(1, domains):
        for core in range(PAIR):
            pl.semaphore_signal(
                barrier,
                inc=1,
                device_id={"aux": lax.rem(domain + turn, domains), "blk": pair_base + core},
                device_id_type=MESH,
            )
    pl.semaphore_wait(barrier, peers - 1 + (domains - 1) * PAIR)

    def source(block, target):
        return x_ref.at[
            :,
            pl.ds(pl.multiple_of(target * SUB, SUB), SUB),
            pl.ds(pl.multiple_of(block * BS, BS), BS),
        ]

    def landing(block, sender):
        return slab.at[block, pl.ds(pl.multiple_of(sender * rows, rows), rows)]

    def outgoing(block, off):
        target = lax.rem(me + off, peers)
        return pltpu.make_async_remote_copy(
            src_ref=source(block, target),
            dst_ref=landing(block, me),
            send_sem=send_sem.at[block, off],
            recv_sem=recv_sem.at[block, off],
            device_id={"blk": target},
            device_id_type=MESH,
        )

    def incoming(block, off):
        sender = lax.rem(me - off + peers, peers)
        return pltpu.make_async_remote_copy(
            src_ref=source(block, me),
            dst_ref=landing(block, sender),
            send_sem=send_sem.at[block, off],
            recv_sem=recv_sem.at[block, off],
            device_id={"blk": sender},
            device_id_type=MESH,
        )

    def own(block):
        return pltpu.make_async_copy(source(block, me), landing(block, me), own_sem.at[block])

    def launch(block, carry):
        def one(off, inner):
            outgoing(block, off).start()
            return inner

        lax.fori_loop(1, peers, one, 0)
        own(block).start()
        return carry

    lax.fori_loop(0, blocks, launch, 0)

    for load in loads:
        load.wait()
    for slot in range(slots):
        gap = abs(slot - (SPAN - 1))
        row = me if slot >= SPAN - 1 else me - gap
        count = jnp.int32(0)
        for index in range(pairs_ref.shape[1]):
            first = pairs_ref[0, index]
            hit = (first == row) & (pairs_ref[1, index] - first == gap)
            count = count + hit.astype(jnp.int32)
        weights[slot] = count.astype(jnp.float32)

    fit_cols[: (SPAN - 1) * BS, :] = jnp.zeros(((SPAN - 1) * BS, SUB * depth), jnp.bfloat16)
    for gap in range(1, SPAN):

        @pl.when(me + gap >= blocks)
        def _():
            sum_in[:, SPAN - 1 + gap] = jnp.zeros((peers, strip, BS), jnp.float32)

    def piece_to(block, off):
        return pltpu.make_async_remote_copy(
            src_ref=piece_out.at[block, lax.rem(place + off, group)],
            dst_ref=piece_in.at[block, place],
            send_sem=piece_send.at[block, off],
            recv_sem=piece_recv.at[block, off],
            device_id=member(off),
            device_id_type=MESH,
        )

    def piece_from(block, off):
        sender = lax.rem(place - off + group, group)
        return pltpu.make_async_remote_copy(
            src_ref=piece_out.at[block, sender],
            dst_ref=piece_in.at[block, sender],
            send_sem=piece_send.at[block, off],
            recv_sem=piece_recv.at[block, off],
            device_id=member(group - off),
            device_id_type=MESH,
        )

    def span_of(gap):
        return pl.ds(0, SPAN) if gap == 0 else pl.ds(SPAN - 1 + gap, 1)

    def sum_to(block, gap):
        return pltpu.make_async_remote_copy(
            src_ref=sum_out.at[block, span_of(gap)],
            dst_ref=sum_in.at[me, span_of(gap)],
            send_sem=sum_send.at[block, gap],
            recv_sem=sum_recv.at[me, gap],
            device_id={"blk": block - gap},
            device_id_type=MESH,
        )

    def sum_from(sender, gap):
        return pltpu.make_async_remote_copy(
            src_ref=sum_out.at[0, span_of(gap)],
            dst_ref=sum_in.at[sender, span_of(gap)],
            send_sem=sum_send.at[0, gap],
            recv_sem=sum_recv.at[sender, gap],
            device_id={"blk": sender},
            device_id_type=MESH,
        )

    def pass_on(block):
        def arrive(off, inner):
            piece_from(block, off).wait_recv()
            return inner

        lax.fori_loop(1, group, arrive, 0)
        total = piece_out[block, place]
        for off in range(1, group):
            total = total + piece_in[block, lax.rem(place + off, group)]
        sum_out[block] = total
        for gap in range(SPAN):
            owner = block - gap

            @pl.when((owner >= 0) & (owner != me))
            def _():
                sum_to(block, gap).start()

            @pl.when(owner == me)
            def _():
                if gap == 0:
                    sum_in[me, :SPAN] = total[:SPAN]
                else:
                    sum_in[me, SPAN - 1 + gap] = total[SPAN - 1 + gap]

    def reorder(block, sender):
        span = pl.ds(pl.multiple_of(sender * rows, rows), rows)
        wide[...] = slab[block, span].reshape(rows * SUB, BS).astype(jnp.float32)
        for i in range(SUB):
            ordered[span, i * BS : (i + 1) * BS] = wide[pl.ds(i, rows, stride=SUB), :].astype(
                jnp.bfloat16
            )

    def step(block, carry):
        @pl.when(block > 0)
        def _():
            pass_on(block - 1)

        def arrive(off, inner):
            incoming(block, off).wait_recv()
            reorder(block, lax.rem(me - off + peers, peers))
            return inner

        own(block).wait()
        reorder(block, me)
        lax.fori_loop(1, peers, arrive, 0)
        for qb in range(depth // QB):
            keep = mask_ref[qb, block].astype(jnp.float32)
            fitted = jnp.dot(
                metric_ref[qb * QB : (qb + 1) * QB, :],
                ordered[...],
                preferred_element_type=jnp.float32,
            )
            fitted = (fitted * keep).astype(jnp.bfloat16)
            for i in range(SUB):
                piece = fitted[:, i * BS : (i + 1) * BS]
                at = i * depth + qb * QB
                fit_rows[at : at + QB, :] = piece
                fit_cols[
                    pl.ds(pl.multiple_of((block + SPAN - 1) * BS, BS), BS), at : at + QB
                ] = piece.T
        tiles = jnp.dot(
            fit_cols[pl.ds(pl.multiple_of(block * BS, BS), SPAN * BS), :],
            fit_rows[...],
            preferred_element_type=jnp.float32,
        )
        for gap in range(SPAN):
            at = (SPAN - 1 - gap) * BS
            tile = tiles[at : at + BS, :]
            piece_out[block, :, SPAN - 1 + gap] = tile.reshape(group, strip, BS)
            if gap > 0:
                piece_out[block, :, SPAN - 1 - gap] = tile.T.reshape(group, strip, BS)

        def one(off, inner):
            piece_to(block, off).start()
            return inner

        lax.fori_loop(1, group, one, 0)
        return carry

    lax.fori_loop(0, blocks, step, 0)
    pass_on(blocks - 1)

    for gap in range(SPAN):

        @pl.when(me + gap < blocks)
        def _():
            def arrive(off, inner):
                sum_from(lax.rem(me + off, peers), gap).wait_recv()
                return inner

            lax.fori_loop(1, peers, arrive, 0)

    for core in range(PAIR):
        for slot in range(slots):
            total = sum_in[core, slot]
            for turn in range(1, peers // PAIR):
                total = total + sum_in[turn * PAIR + core, slot]
            out_ref[0, core * strip : (core + 1) * strip, slot * BS : (slot + 1) * BS] = (
                total * weights[slot]
            )

    def settle(block, carry):
        def one(off, inner):
            outgoing(block, off).wait_send()
            return inner

        def two(off, inner):
            piece_to(block, off).wait_send()
            return inner

        lax.fori_loop(1, peers, one, 0)
        lax.fori_loop(1, group, two, 0)
        for gap in range(SPAN):
            owner = block - gap

            @pl.when((owner >= 0) & (owner != me))
            def _():
                sum_to(block, gap).wait_send()

        return carry

    lax.fori_loop(0, blocks, settle, 0)


def by_orbital(integrals, metric, pair_list, aux_mask):
    peers = lax.axis_size("blk")
    domains = lax.axis_size("aux")
    depth = metric.shape[1]
    blocks = aux_mask.shape[1]
    group = domains * PAIR
    slots = 2 * SPAN - 1
    strip = BS // group
    return pl.pallas_call(
        functools.partial(tile_kernel, peers, domains, blocks, depth),
        out_shape=jax.ShapeDtypeStruct((1, BS // domains, slots * BS), jnp.float32),
        in_specs=[
            pl.BlockSpec(memory_space=pl.ANY),
            pl.BlockSpec(memory_space=pl.ANY),
            pl.BlockSpec(memory_space=pl.ANY),
            pl.BlockSpec(memory_space=pl.ANY),
        ],
        out_specs=pl.BlockSpec(memory_space=pltpu.VMEM),
        scratch_shapes=[
            pltpu.SMEM(aux_mask.shape, jnp.int32),
            pltpu.SMEM(pair_list.shape[::-1], jnp.int32),
            pltpu.VMEM(metric.shape, jnp.bfloat16),
            pltpu.VMEM((blocks, depth, SUB, BS), jnp.bfloat16),
            pltpu.VMEM((depth // peers * SUB, BS), jnp.float32),
            pltpu.VMEM((depth, SUB * BS), jnp.bfloat16),
            pltpu.VMEM((SUB * depth, BS), jnp.bfloat16),
            pltpu.VMEM(((blocks + SPAN - 1) * BS, SUB * depth), jnp.bfloat16),
            pltpu.VMEM((blocks, group, slots, strip, BS), jnp.float32),
            pltpu.VMEM((blocks, group, slots, strip, BS), jnp.float32),
            pltpu.VMEM((blocks, slots, strip, BS), jnp.float32),
            pltpu.VMEM((peers, slots, strip, BS), jnp.float32),
            pltpu.SMEM((slots,), jnp.float32),
            pltpu.SemaphoreType.DMA((blocks, peers)),
            pltpu.SemaphoreType.DMA((blocks, peers)),
            pltpu.SemaphoreType.DMA((blocks,)),
            pltpu.SemaphoreType.DMA((blocks, group)),
            pltpu.SemaphoreType.DMA((blocks, group)),
            pltpu.SemaphoreType.DMA((blocks, SPAN)),
            pltpu.SemaphoreType.DMA((peers, SPAN)),
            pltpu.SemaphoreType.DMA((3,)),
        ],
        compiler_params=pltpu.CompilerParams(
            collective_id=0, has_side_effects=True, vmem_limit_bytes=60 * 1024 * 1024
        ),
    )(aux_mask, pair_list.T, metric, integrals)


def from_behind(array, axis, by):
    peers = lax.axis_size(axis)
    pairs = [(i, i + by) for i in range(peers) if 0 <= i + by < peers]
    return lax.ppermute(array, axis, pairs)


def fit_block(metric, slab_piece, mask_rows):
    fitted = jnp.einsum("pq,qjn->pjn", metric, slab_piece, preferred_element_type=jnp.float32)
    return (fitted * mask_rows[:, None, None]).astype(jnp.bfloat16)


def by_block(integrals, metric, pair_list, aux_mask):
    block_count = aux_mask.shape[1]
    position = lax.axis_index("blk")
    block_ids = jnp.arange(block_count, dtype=jnp.int32)
    offsets = jnp.arange(SPAN, dtype=jnp.int32)
    col_gap = pair_list[:, 1] - pair_list[:, 0]
    hits = (pair_list[:, 0][:, None] == position) & (col_gap[:, None] == offsets[None, :])
    listed = jnp.sum(hits.astype(jnp.int32), axis=0)
    one_hot = (block_ids == position).astype(jnp.int32)
    column = jnp.sum(aux_mask * one_hot[None, :], axis=1)
    own_mask = jnp.repeat(column, QB).astype(jnp.float32)
    own_block = fit_block(
        metric, lax.all_to_all(integrals, "blk", split_axis=2, concat_axis=0, tiled=True), own_mask
    )
    partners = [own_block]
    current = own_block
    for turn_index in range(SPAN - 1):
        current = from_behind(current, "blk", -1)
        partners.append(current)
    flat_own = partners[0].reshape(-1, BS)

    def make_tile(partner):
        return lax.dot_general(
            flat_own,
            partner.reshape(-1, BS),
            (((0,), (0,)), ((), ())),
            preferred_element_type=jnp.float32,
        )

    tile_list = [
        make_tile(partners[offset]) * listed[offset].astype(jnp.float32) for offset in range(SPAN)
    ]
    upper_tiles = jnp.stack(tile_list)
    mirror_tiles = jnp.stack([jnp.transpose(tile_list[offset]) for offset in range(1, SPAN)])
    lower_tiles = []
    moving = mirror_tiles
    for turn_index in range(SPAN - 1):
        moving = from_behind(moving.astype(jnp.bfloat16), "blk", 1).astype(moving.dtype)
        lower_tiles.append(moving[0])
        moving = moving[1:]
    whole_band = jnp.concatenate(
        [jnp.stack([lower_tiles[SPAN - 2 - slot] for slot in range(SPAN - 1)]), upper_tiles], axis=0
    )
    band_parts = lax.psum_scatter(whole_band, "aux", scatter_dimension=1, tiled=True)
    pieces = [band_parts[slot] for slot in range(2 * SPAN - 1)]
    band_rows = jnp.concatenate(pieces, axis=1)
    return band_rows[None]


def local(integrals, metric, pair_list, aux_mask):
    peers = lax.axis_size("blk")
    blocks = aux_mask.shape[1]
    strips = BS % (8 * PAIR * lax.axis_size("aux")) == 0 and peers % PAIR == 0
    whole_tiles = integrals.shape[1] == SUB * peers and blocks == peers and strips
    if whole_tiles:
        return by_orbital(integrals, metric, pair_list, aux_mask)
    return by_block(integrals, metric, pair_list, aux_mask)


def solution(mesh):
    return jax.shard_map(
        local,
        mesh=mesh,
        in_specs=(P(("aux", "blk"), None, None), P("aux", None), P(), P("aux", None)),
        out_specs=P("blk", "aux", None),
        check_vma=False,
    )
```

```python
import functools

import jax
import jax.numpy as jnp
from jax import lax
from jax.experimental import pallas as pl
from jax.experimental.pallas import tpu as pltpu
from jax.sharding import PartitionSpec as P

BS = 128
QB = 128
SPAN = 3
SUB = 8
PAIR = 2
MESH = pl.DeviceIdType.MESH


def tile_kernel(
    peers, domains, blocks, depth, mask_hbm, pairs_hbm, metric_hbm, x_ref, out_ref,
    mask_ref, pairs_ref, metric_ref,
    slab, wide, ordered, fit_rows, fit_cols, piece_out, piece_in, sum_out, sum_in, weights,
    send_sem, recv_sem, own_sem, piece_send, piece_recv, sum_send, sum_recv, load_sem,
):
    me = lax.axis_index("blk")
    domain = lax.axis_index("aux")
    rows = depth // peers
    group = domains * PAIR
    strip = BS // group
    pair_base = (me // PAIR) * PAIR
    place = domain * PAIR + lax.rem(me, PAIR)
    slots = 2 * SPAN - 1

    loads = [
        pltpu.make_async_copy(mask_hbm, mask_ref, load_sem.at[0]),
        pltpu.make_async_copy(pairs_hbm, pairs_ref, load_sem.at[1]),
        pltpu.make_async_copy(metric_hbm, metric_ref, load_sem.at[2]),
    ]
    for load in loads:
        load.start()
    barrier = pltpu.get_barrier_semaphore()

    def member(off):
        other = lax.rem(place + off, group)
        return {"aux": other // PAIR, "blk": pair_base + lax.rem(other, PAIR)}

    def greet(off, carry):
        pl.semaphore_signal(
            barrier, inc=1, device_id={"blk": lax.rem(me + off, peers)}, device_id_type=MESH
        )
        return carry

    lax.fori_loop(1, peers, greet, 0)
    for turn in range(1, domains):
        for core in range(PAIR):
            pl.semaphore_signal(
                barrier,
                inc=1,
                device_id={"aux": lax.rem(domain + turn, domains), "blk": pair_base + core},
                device_id_type=MESH,
            )
    pl.semaphore_wait(barrier, peers - 1 + (domains - 1) * PAIR)

    def source(block, target):
        return x_ref.at[
            :,
            pl.ds(pl.multiple_of(target * SUB, SUB), SUB),
            pl.ds(pl.multiple_of(block * BS, BS), BS),
        ]

    def landing(block, sender):
        return slab.at[block, pl.ds(pl.multiple_of(sender * rows, rows), rows)]

    def outgoing(block, off):
        target = lax.rem(me + off, peers)
        return pltpu.make_async_remote_copy(
            src_ref=source(block, target),
            dst_ref=landing(block, me),
            send_sem=send_sem.at[block, off],
            recv_sem=recv_sem.at[block, off],
            device_id={"blk": target},
            device_id_type=MESH,
        )

    def incoming(block, off):
        sender = lax.rem(me - off + peers, peers)
        return pltpu.make_async_remote_copy(
            src_ref=source(block, me),
            dst_ref=landing(block, sender),
            send_sem=send_sem.at[block, off],
            recv_sem=recv_sem.at[block, off],
            device_id={"blk": sender},
            device_id_type=MESH,
        )

    def own(block):
        return pltpu.make_async_copy(source(block, me), landing(block, me), own_sem.at[block])

    def launch(block, carry):
        def one(off, inner):
            outgoing(block, off).start()
            return inner

        lax.fori_loop(1, peers, one, 0)
        own(block).start()
        return carry

    lax.fori_loop(0, blocks, launch, 0)

    for load in loads:
        load.wait()
    for slot in range(slots):
        gap = abs(slot - (SPAN - 1))
        row = me if slot >= SPAN - 1 else me - gap
        count = jnp.int32(0)
        for index in range(pairs_ref.shape[1]):
            first = pairs_ref[0, index]
            hit = (first == row) & (pairs_ref[1, index] - first == gap)
            count = count + hit.astype(jnp.int32)
        weights[slot] = count.astype(jnp.float32)

    fit_cols[: (SPAN - 1) * BS, :] = jnp.zeros(((SPAN - 1) * BS, SUB * depth), jnp.bfloat16)
    for gap in range(1, SPAN):

        @pl.when(me + gap >= blocks)
        def _():
            sum_in[:, SPAN - 1 + gap] = jnp.zeros((peers, strip, BS), jnp.float32)

    def piece_to(block, off):
        return pltpu.make_async_remote_copy(
            src_ref=piece_out.at[block, lax.rem(place + off, group)],
            dst_ref=piece_in.at[block, place],
            send_sem=piece_send.at[block, off],
            recv_sem=piece_recv.at[block, off],
            device_id=member(off),
            device_id_type=MESH,
        )

    def piece_from(block, off):
        sender = lax.rem(place - off + group, group)
        return pltpu.make_async_remote_copy(
            src_ref=piece_out.at[block, sender],
            dst_ref=piece_in.at[block, sender],
            send_sem=piece_send.at[block, off],
            recv_sem=piece_recv.at[block, off],
            device_id=member(group - off),
            device_id_type=MESH,
        )

    def span_of(gap):
        return pl.ds(0, SPAN) if gap == 0 else pl.ds(SPAN - 1 + gap, 1)

    def sum_to(block, gap):
        return pltpu.make_async_remote_copy(
            src_ref=sum_out.at[block, span_of(gap)],
            dst_ref=sum_in.at[me, span_of(gap)],
            send_sem=sum_send.at[block, gap],
            recv_sem=sum_recv.at[me, gap],
            device_id={"blk": block - gap},
            device_id_type=MESH,
        )

    def sum_from(sender, gap):
        return pltpu.make_async_remote_copy(
            src_ref=sum_out.at[0, span_of(gap)],
            dst_ref=sum_in.at[sender, span_of(gap)],
            send_sem=sum_send.at[0, gap],
            recv_sem=sum_recv.at[sender, gap],
            device_id={"blk": sender},
            device_id_type=MESH,
        )

    def pass_on(block):
        def arrive(off, inner):
            piece_from(block, off).wait_recv()
            return inner

        lax.fori_loop(1, group, arrive, 0)
        total = piece_out[block, place]
        for off in range(1, group):
            total = total + piece_in[block, lax.rem(place + off, group)]
        sum_out[block] = total
        for gap in range(SPAN):
            owner = block - gap

            @pl.when(owner == me)
            def _():
                if gap == 0:
                    sum_in[me, :SPAN] = total[:SPAN]
                else:
                    sum_in[me, SPAN - 1 + gap] = total[SPAN - 1 + gap]

    def ship(block, carry):
        for gap in range(SPAN):
            owner = block - gap

            @pl.when((owner >= 0) & (owner != me))
            def _():
                sum_to(block, gap).start()

        return carry

    def reorder(block, sender):
        span = pl.ds(pl.multiple_of(sender * rows, rows), rows)
        wide[...] = slab[block, span].reshape(rows * SUB, BS).astype(jnp.float32)
        for i in range(SUB):
            ordered[span, i * BS : (i + 1) * BS] = wide[pl.ds(i, rows, stride=SUB), :].astype(
                jnp.bfloat16
            )

    def step(block, carry):
        @pl.when(block > 0)
        def _():
            pass_on(block - 1)

        def arrive(off, inner):
            incoming(block, off).wait_recv()
            reorder(block, lax.rem(me - off + peers, peers))
            return inner

        own(block).wait()
        reorder(block, me)
        lax.fori_loop(1, peers, arrive, 0)

        @pl.when(block == blocks - 1)
        def _():
            lax.fori_loop(0, blocks - 1, ship, 0)

        for qb in range(depth // QB):
            keep = mask_ref[qb, block].astype(jnp.float32)
            fitted = jnp.dot(
                metric_ref[qb * QB : (qb + 1) * QB, :],
                ordered[...],
                preferred_element_type=jnp.float32,
            )
            fitted = (fitted * keep).astype(jnp.bfloat16)
            for i in range(SUB):
                piece = fitted[:, i * BS : (i + 1) * BS]
                at = i * depth + qb * QB
                fit_rows[at : at + QB, :] = piece
                fit_cols[
                    pl.ds(pl.multiple_of((block + SPAN - 1) * BS, BS), BS), at : at + QB
                ] = piece.T
        tiles = jnp.dot(
            fit_cols[pl.ds(pl.multiple_of(block * BS, BS), SPAN * BS), :],
            fit_rows[...],
            preferred_element_type=jnp.float32,
        )
        for gap in range(SPAN):
            at = (SPAN - 1 - gap) * BS
            tile = tiles[at : at + BS, :]
            piece_out[block, :, SPAN - 1 + gap] = tile.reshape(group, strip, BS)
            if gap > 0:
                piece_out[block, :, SPAN - 1 - gap] = tile.T.reshape(group, strip, BS)

        def one(off, inner):
            piece_to(block, off).start()
            return inner

        lax.fori_loop(1, group, one, 0)
        return carry

    lax.fori_loop(0, blocks, step, 0)
    pass_on(blocks - 1)
    ship(blocks - 1, 0)

    for gap in range(SPAN):

        @pl.when(me + gap < blocks)
        def _():
            def arrive(off, inner):
                sum_from(lax.rem(me + off, peers), gap).wait_recv()
                return inner

            lax.fori_loop(1, peers, arrive, 0)

    for core in range(PAIR):
        for slot in range(slots):
            total = sum_in[core, slot]
            for turn in range(1, peers // PAIR):
                total = total + sum_in[turn * PAIR + core, slot]
            out_ref[0, core * strip : (core + 1) * strip, slot * BS : (slot + 1) * BS] = (
                total * weights[slot]
            )

    def settle(block, carry):
        def one(off, inner):
            outgoing(block, off).wait_send()
            return inner

        def two(off, inner):
            piece_to(block, off).wait_send()
            return inner

        lax.fori_loop(1, peers, one, 0)
        lax.fori_loop(1, group, two, 0)
        for gap in range(SPAN):
            owner = block - gap

            @pl.when((owner >= 0) & (owner != me))
            def _():
                sum_to(block, gap).wait_send()

        return carry

    lax.fori_loop(0, blocks, settle, 0)


def in_hbm(operand):
    return pltpu.with_memory_space_constraint(operand, pltpu.MemorySpace.HBM)


def by_orbital(integrals, metric, pair_list, aux_mask):
    peers = lax.axis_size("blk")
    domains = lax.axis_size("aux")
    depth = metric.shape[1]
    blocks = aux_mask.shape[1]
    group = domains * PAIR
    slots = 2 * SPAN - 1
    strip = BS // group
    return pl.pallas_call(
        functools.partial(tile_kernel, peers, domains, blocks, depth),
        out_shape=jax.ShapeDtypeStruct((1, BS // domains, slots * BS), jnp.float32),
        in_specs=[
            pl.BlockSpec(memory_space=pl.ANY),
            pl.BlockSpec(memory_space=pl.ANY),
            pl.BlockSpec(memory_space=pl.ANY),
            pl.BlockSpec(memory_space=pl.ANY),
        ],
        out_specs=pl.BlockSpec(memory_space=pltpu.VMEM),
        scratch_shapes=[
            pltpu.SMEM(aux_mask.shape, jnp.int32),
            pltpu.SMEM(pair_list.shape[::-1], jnp.int32),
            pltpu.VMEM(metric.shape, jnp.bfloat16),
            pltpu.VMEM((blocks, depth, SUB, BS), jnp.bfloat16),
            pltpu.VMEM((depth // peers * SUB, BS), jnp.float32),
            pltpu.VMEM((depth, SUB * BS), jnp.bfloat16),
            pltpu.VMEM((SUB * depth, BS), jnp.bfloat16),
            pltpu.VMEM(((blocks + SPAN - 1) * BS, SUB * depth), jnp.bfloat16),
            pltpu.VMEM((blocks, group, slots, strip, BS), jnp.float32),
            pltpu.VMEM((blocks, group, slots, strip, BS), jnp.float32),
            pltpu.VMEM((blocks, slots, strip, BS), jnp.float32),
            pltpu.VMEM((peers, slots, strip, BS), jnp.float32),
            pltpu.SMEM((slots,), jnp.float32),
            pltpu.SemaphoreType.DMA((blocks, peers)),
            pltpu.SemaphoreType.DMA((blocks, peers)),
            pltpu.SemaphoreType.DMA((blocks,)),
            pltpu.SemaphoreType.DMA((blocks, group)),
            pltpu.SemaphoreType.DMA((blocks, group)),
            pltpu.SemaphoreType.DMA((blocks, SPAN)),
            pltpu.SemaphoreType.DMA((peers, SPAN)),
            pltpu.SemaphoreType.DMA((3,)),
        ],
        compiler_params=pltpu.CompilerParams(
            collective_id=0, has_side_effects=True, vmem_limit_bytes=36 * 1024 * 1024
        ),
    )(*[in_hbm(operand) for operand in (aux_mask, pair_list.T, metric, integrals)])


def from_behind(array, axis, by):
    peers = lax.axis_size(axis)
    pairs = [(i, i + by) for i in range(peers) if 0 <= i + by < peers]
    return lax.ppermute(array, axis, pairs)


def fit_block(metric, slab_piece, mask_rows):
    fitted = jnp.einsum("pq,qjn->pjn", metric, slab_piece, preferred_element_type=jnp.float32)
    return (fitted * mask_rows[:, None, None]).astype(jnp.bfloat16)


def by_block(integrals, metric, pair_list, aux_mask):
    block_count = aux_mask.shape[1]
    position = lax.axis_index("blk")
    block_ids = jnp.arange(block_count, dtype=jnp.int32)
    offsets = jnp.arange(SPAN, dtype=jnp.int32)
    col_gap = pair_list[:, 1] - pair_list[:, 0]
    hits = (pair_list[:, 0][:, None] == position) & (col_gap[:, None] == offsets[None, :])
    listed = jnp.sum(hits.astype(jnp.int32), axis=0)
    one_hot = (block_ids == position).astype(jnp.int32)
    column = jnp.sum(aux_mask * one_hot[None, :], axis=1)
    own_mask = jnp.repeat(column, QB).astype(jnp.float32)
    own_block = fit_block(
        metric, lax.all_to_all(integrals, "blk", split_axis=2, concat_axis=0, tiled=True), own_mask
    )
    partners = [own_block]
    current = own_block
    for turn_index in range(SPAN - 1):
        current = from_behind(current, "blk", -1)
        partners.append(current)
    flat_own = partners[0].reshape(-1, BS)

    def make_tile(partner):
        return lax.dot_general(
            flat_own,
            partner.reshape(-1, BS),
            (((0,), (0,)), ((), ())),
            preferred_element_type=jnp.float32,
        )

    tile_list = [
        make_tile(partners[offset]) * listed[offset].astype(jnp.float32) for offset in range(SPAN)
    ]
    upper_tiles = jnp.stack(tile_list)
    mirror_tiles = jnp.stack([jnp.transpose(tile_list[offset]) for offset in range(1, SPAN)])
    lower_tiles = []
    moving = mirror_tiles
    for turn_index in range(SPAN - 1):
        moving = from_behind(moving.astype(jnp.bfloat16), "blk", 1).astype(moving.dtype)
        lower_tiles.append(moving[0])
        moving = moving[1:]
    whole_band = jnp.concatenate(
        [jnp.stack([lower_tiles[SPAN - 2 - slot] for slot in range(SPAN - 1)]), upper_tiles], axis=0
    )
    band_parts = lax.psum_scatter(whole_band, "aux", scatter_dimension=1, tiled=True)
    pieces = [band_parts[slot] for slot in range(2 * SPAN - 1)]
    band_rows = jnp.concatenate(pieces, axis=1)
    return band_rows[None]


def local(integrals, metric, pair_list, aux_mask):
    peers = lax.axis_size("blk")
    blocks = aux_mask.shape[1]
    strips = BS % (8 * PAIR * lax.axis_size("aux")) == 0 and peers % PAIR == 0
    whole_tiles = integrals.shape[1] == SUB * peers and blocks == peers and strips
    if whole_tiles:
        return by_orbital(integrals, metric, pair_list, aux_mask)
    return by_block(integrals, metric, pair_list, aux_mask)


def solution(mesh):
    return jax.shard_map(
        local,
        mesh=mesh,
        in_specs=(P(("aux", "blk"), None, None), P("aux", None), P(), P("aux", None)),
        out_specs=P("blk", "aux", None),
        check_vma=False,
    )
```
